512 devices in a mesh: section: 8 (over x, core), seq: 16 (over z), chan: 4 (over y).
Axes of the slice: x: 4, y: 4, z: 16, core: 2. Of those that a mesh axis runs over, the one named last changes fastest.
Arguments:
- saved_input: bfloat16 [8, 2, 2048, 1024], P('section', None, 'seq', 'chan'), may hold values from -6 to 6
- pre_gate: bfloat16 [8, 2, 2048, 1024], P('section', None, 'seq', 'chan'), may hold values from -6 to 6
- post_gate: bfloat16 [8, 2, 2048, 1024], P('section', None, 'seq', 'chan'), may hold values from -6 to 6
- grad_held: bfloat16 [8, 2048, 1024], P('section', 'seq', 'chan'), may hold values from -6 to 6
- loss_grad: bfloat16 [2048, 1024], P('seq', 'chan'), may hold values from -6 to 6
- filters: float32 [8, 2048, 256], P('section', 'seq'), may hold values from -1 to 1
- skip_gain: float32 [8, 256], P('section'), may hold values from 0.5 to 1.5
Outputs:
- grad_out: bfloat16 [8, 2048, 1024], P('section', 'seq', 'chan')
- filter_grad: float32 [8, 2048, 256], P('section', 'seq', 'chan')
The draws below stay inside these ranges and needn't reach their ends.
All inputs are finite; a program needn't handle non-finite values.
Results may differ from the reference program's by a relative error of at most 0.017.
Values may be sent and summed in bfloat16 or wider, within the bound.
A program may use at most 64 MiB of HBM per device.

```python
import math
import jax
import jax.numpy as jnp
from jax import lax

CH = 256
TICKS = 2
SECTIONS = 8
LEN = 2048
WIDTH = 1024


def draw_filters(key, part):
    key_rate = jax.random.fold_in(key, 11)
    key_noise = jax.random.fold_in(key, 23)
    position = jnp.arange(LEN, dtype=jnp.float32)[None, :, None]
    decay_rate = jnp.exp(jax.random.uniform(key_rate, (SECTIONS, 1, CH), jnp.float32, math.log(0.3), math.log(LEN / 40.0)))
    noise_values = jnp.clip(jax.random.normal(key_noise, (SECTIONS, LEN, CH), jnp.float32), -4.0, 4.0)
    envelope = jnp.exp(-decay_rate * position / LEN)
    energy = -jnp.expm1(-2.0 * decay_rate) / -jnp.expm1(-2.0 * decay_rate / LEN)
    return noise_values * envelope / jnp.sqrt(energy)


def block_levels(stream_key, shape, pieces, smallest, high):
    def one(axis_at, blocks):
        draws = jax.random.uniform(jax.random.fold_in(jax.random.fold_in(stream_key, 6), axis_at), (blocks,), jnp.float32, smallest / len(pieces), high / len(pieces))
        return jnp.repeat(jnp.exp(draws), shape[axis_at] // blocks).reshape((-1,) + (1,) * (len(shape) - axis_at - 1))

    loudness = one(*pieces[0])
    for cut in pieces[1:]:
        loudness = loudness * one(*cut)
    return loudness


def bell_draw(key, dims, scale, most, shards=(), kind=jnp.bfloat16):
    gain = block_levels(key, dims, shards, -0.22, 0.18) if shards else 1.0
    entries = jax.random.normal(key, dims, jnp.float32) * scale * gain
    return jnp.minimum(jnp.maximum(entries, -most), most).astype(kind)


def setup_inputs(seed: int = 0) -> dict:
    seeds = jax.random.split(jax.random.key(seed), 8)
    saved_input = bell_draw(seeds[0], (SECTIONS, TICKS, LEN, WIDTH), 1.0, 6.0, ((0, 8), (2, 16), (3, 4)))
    pre_gate = bell_draw(seeds[1], (SECTIONS, TICKS, LEN, WIDTH), 1.0, 6.0, ((0, 8), (2, 16), (3, 4)))
    post_gate = bell_draw(seeds[2], (SECTIONS, TICKS, LEN, WIDTH), 1.0, 6.0, ((0, 8), (2, 16), (3, 4)))
    grad_held = bell_draw(seeds[3], (SECTIONS, LEN, WIDTH), 1.0, 6.0, ((0, 8), (1, 16), (2, 4)))
    loss_grad = bell_draw(seeds[4], (LEN, WIDTH), 1.0, 6.0, ((0, 16), (1, 4)))
    filters = draw_filters(jax.random.fold_in(seeds[7], 71), 0)
    skip_gain = jnp.clip(0.5 + 1.0 * jax.random.uniform(seeds[6], (SECTIONS, CH), jnp.float32) ** block_levels(seeds[6], (SECTIONS, CH), ((0, 8),), -0.2, 0.2), 0.5, 1.5)
    return dict(saved_input=saved_input, pre_gate=pre_gate, post_gate=post_gate, grad_held=grad_held, loss_grad=loss_grad, filters=filters, skip_gain=skip_gain)


def reference(saved_input, pre_gate, post_gate, grad_held, loss_grad, filters, skip_gain):
    section_count, tick_count, seq_length, width_all = saved_input.shape
    channel_count = filters.shape[2]
    slab_count = width_all // channel_count
    padded = 2 * seq_length
    kernel = jnp.tile(filters, (1, 1, slab_count))
    skip_full = jnp.tile(skip_gain, (1, slab_count))
    kernel_spec = jnp.fft.fft(kernel, n=padded, axis=1)
    carried = [grad_held[section_index].astype(jnp.float32) for section_index in range(section_count)]
    sums_list = [jnp.zeros((padded, width_all), dtype=kernel_spec.dtype) for section_index in range(section_count)]
    produced = []
    for tick_step in range(tick_count):
        produced = []
        new_sums = []
        for section_index in range(section_count):
            gate_in = pre_gate[section_index, tick_step].astype(jnp.float32)
            mixed_input = gate_in * saved_input[section_index, tick_step].astype(jnp.float32)
            gated_grad = post_gate[section_index, tick_step].astype(jnp.float32) * carried[section_index]
            gated_spec = jnp.fft.fft(gated_grad, n=padded, axis=0)
            mixed_spec = jnp.fft.fft(mixed_input, n=padded, axis=0)
            correlated = jnp.real(jnp.fft.ifft(jnp.conj(kernel_spec[section_index]) * gated_spec, axis=0))[:seq_length]
            gradient = (carried[section_index] + gate_in * (correlated + skip_full[section_index] * gated_grad)).astype(jnp.bfloat16)
            new_sums.append(sums_list[section_index] + gated_spec * jnp.conj(mixed_spec))
            produced.append(gradient)
        sums_list = new_sums
        if tick_step + 1 < tick_count:
            carried = [produced[section_index + 1].astype(jnp.float32) for section_index in range(section_count - 1)]
            carried = carried + [loss_grad.astype(jnp.float32)]
    grad_out = jnp.stack(produced)
    grad_scale = 1.0 / math.sqrt(seq_length * slab_count * tick_count)
    lag_list = []
    for section_index in range(section_count):
        lag_full = jnp.real(jnp.fft.ifft(sums_list[section_index], axis=0))[:seq_length]
        lag_list.append(lax.optimization_barrier(jnp.sum(lag_full.reshape(seq_length, slab_count, channel_count), axis=1)))
    filter_grad = (jnp.stack(lag_list) * grad_scale).astype(jnp.float32)
    return (grad_out, filter_grad)
```

```python
import functools
import math

import jax
import jax.numpy as jnp
from jax import lax
from jax.experimental import pallas as pl
from jax.experimental.pallas import tpu as pltpu
from jax.sharding import PartitionSpec as P

LANES = 128


def kernel(
    sections,
    n,
    chans,
    scale,
    saved,
    pre,
    post,
    grad_held,
    loss_grad,
    filters,
    gain,
    grad_out,
    filter_out,
    send_a,
    recv_a,
    send_b,
    recv_b,
    send_c,
    recv_c,
    send_d,
    recv_d,
    send_e,
    recv_e,
    send_f,
    recv_f,
    send_g,
    recv_g,
    carried,
    rows,
    padded,
    left,
    hankel,
    result,
    partial,
    send_sem,
    recv_sem,
    shift_sem,
):
    section = lax.axis_index("section")
    me = lax.axis_index("seq")
    chan = lax.axis_index("chan")
    width = grad_held.shape[1]
    own = width // n
    per_chan = n // chans
    owner_chan = me // per_chan
    keeps_own = owner_chan == chan
    order = sorted(range(1, n), key=lambda off: -min(off, n - off))

    barrier = pltpu.get_barrier_semaphore()
    for off in order:
        pl.semaphore_signal(barrier, inc=1, device_id={"seq": lax.rem(me + off, n)})

    @pl.when(section < sections - 1)
    def _():
        pl.semaphore_signal(barrier, inc=1, device_id={"section": section + 1})

    for slot in range(n):
        source = chan * per_chan + slot // chans

        @pl.when(jnp.logical_not((source == me) & (slot % chans == chan)))
        def _():
            pl.semaphore_signal(
                barrier, inc=1, device_id={"seq": source, "chan": jnp.int32(slot % chans)}
            )

    row_index = lax.broadcasted_iota(jnp.int32, (LANES, LANES), 0)
    lane_index = lax.broadcasted_iota(jnp.int32, (LANES, LANES), 1)
    flip = (row_index + lane_index == LANES - 1).astype(jnp.bfloat16)
    keep = lane_index <= row_index

    def by_channel(values):
        return jnp.transpose(values).astype(jnp.bfloat16)

    def flipped(values):
        turned = jnp.dot(by_channel(values), flip, preferred_element_type=jnp.float32)
        return turned.astype(jnp.bfloat16)

    gated_0 = post[0].astype(jnp.float32) * grad_held[...].astype(jnp.float32)
    send_a[:, 0] = by_channel(gated_0).reshape(n, own, LANES)
    send_a[:, 1] = flipped(filters[...]).reshape(n, own, LANES)
    for tick in range(2):
        mixed = pre[tick].astype(jnp.float32) * saved[tick].astype(jnp.float32)
        send_b[:, tick] = flipped(mixed).reshape(n, own, LANES)

    def exchange(src, dst, phase):
        copies = []
        for off in order:
            peer = lax.rem(me + off, n)
            copy = pltpu.make_async_remote_copy(
                src_ref=src.at[peer],
                dst_ref=dst.at[me],
                send_sem=send_sem.at[phase, off],
                recv_sem=recv_sem.at[phase, off],
                device_id={"seq": peer},
            )
            copy.start()
            copies.append(copy)
        dst[me] = src[me]
        return copies

    waiting = (
        n - 1 + n + (section > 0).astype(jnp.int32) - keeps_own.astype(jnp.int32)
    )
    pl.semaphore_wait(barrier, waiting)

    sent = []

    def arrive(copies):
        for copy in copies:
            copy.wait_recv()
        sent.extend(copies)

    def build_left(block, which):
        for m in range(n):
            padded[:, n - 1 - m, :] = block(m).astype(jnp.float32)

        def one(ch, carry):
            for m in range(n):
                left[which, ch, :, m * LANES : (m + 1) * LANES] = padded[
                    ch, n - 1 - m : 2 * n - 1 - m, :
                ].astype(jnp.bfloat16)
            return carry

        lax.fori_loop(0, own, one, 0)

    def correlate(block, send):
        for m in range(n):
            rows[:, m, :] = block(m).astype(jnp.float32)

        def one(ch, carry):
            held = rows[ch]

            def turned(m):
                spread = jnp.broadcast_to(held[m : m + 1], (LANES, LANES))
                return pltpu.roll(spread, 1, 1, stride=1, stride_axis=0)

            now = turned(0)
            for m in range(n):
                later = turned(m + 1) if m + 1 < n else jnp.zeros_like(now)
                hankel[ch, m * LANES : (m + 1) * LANES, :] = jnp.where(
                    keep, now, later
                ).astype(jnp.bfloat16)
                now = later
            result[ch] = jnp.dot(left[0, ch], hankel[ch], preferred_element_type=jnp.float32)
            return carry

        lax.fori_loop(0, own, one, 0)
        for m in range(n):
            send[m] = result[:, m, :].astype(jnp.bfloat16)

    def lag_products(tick):
        def one(ch, carry):
            product = jnp.dot(
                left[1 + tick, ch], hankel[ch], preferred_element_type=jnp.float32
            )
            if tick == 0:
                partial[ch] = product
            else:
                partial[ch] = partial[ch] + product
            return carry

        lax.fori_loop(0, own, one, 0)

    def combined(tick, held, gated, recv):
        back = jnp.transpose(recv[...].astype(jnp.float32).reshape(width, LANES))
        inner = back + gain[...] * gated
        return (held + pre[tick].astype(jnp.float32) * inner).astype(jnp.bfloat16)

    copies_a = exchange(send_a, recv_a, 0)
    copies_b = exchange(send_b, recv_b, 1)
    padded[:, n:, :] = jnp.zeros((own, n, LANES), jnp.float32)
    arrive(copies_a)
    build_left(lambda m: recv_a[m, 1], 0)
    correlate(lambda m: recv_a[m, 0], send_c)
    copies_c = exchange(send_c, recv_c, 2)
    arrive(copies_b)
    build_left(lambda m: recv_b[m, 0], 1)
    lag_products(0)
    arrive(copies_c)
    send_g[...] = combined(0, grad_held[...].astype(jnp.float32), gated_0, recv_c)
    shift = pltpu.make_async_remote_copy(
        src_ref=send_g,
        dst_ref=recv_g,
        send_sem=shift_sem.at[0],
        recv_sem=shift_sem.at[1],
        device_id={"section": lax.rem(section + sections - 1, sections)},
    )

    @pl.when(section > 0)
    def _():
        shift.start()

    build_left(lambda m: recv_b[m, 1], 2)

    @pl.when(section < sections - 1)
    def _():
        shift.wait_recv()
        carried[...] = recv_g[...].astype(jnp.float32)

    @pl.when(section == sections - 1)
    def _():
        carried[...] = loss_grad[...].astype(jnp.float32)

    gated_1 = post[1].astype(jnp.float32) * carried[...]
    send_d[...] = by_channel(gated_1).reshape(n, own, LANES)
    copies_d = exchange(send_d, recv_d, 3)
    arrive(copies_d)
    correlate(lambda m: recv_d[m], send_e)
    copies_e = exchange(send_e, recv_e, 4)
    lag_products(1)
    for m in range(n):
        send_f[m] = partial[:, m, :].astype(jnp.bfloat16)

    landing = lax.rem(me, per_chan) * chans + chan

    def deliver(off):
        target = lax.rem(me + off, n)
        return pltpu.make_async_remote_copy(
            src_ref=send_f.at[target],
            dst_ref=recv_f.at[landing],
            send_sem=send_sem.at[5, off],
            recv_sem=recv_sem.at[5, landing],
            device_id={"seq": target, "chan": owner_chan},
        )

    for off in order:
        deliver(off).start()

    @pl.when(jnp.logical_not(keeps_own))
    def _():
        deliver(0).start()

    @pl.when(keeps_own)
    def _():
        recv_f[landing] = send_f[me]

    arrive(copies_e)
    grad_out[...] = combined(1, carried[...], gated_1, recv_e)

    for slot in range(n):
        source = chan * per_chan + slot // chans

        @pl.when(jnp.logical_not((source == me) & (slot % chans == chan)))
        def _():
            pltpu.make_async_remote_copy(
                src_ref=send_f.at[0],
                dst_ref=recv_f.at[slot],
                send_sem=send_sem.at[5, 0],
                recv_sem=recv_sem.at[5, slot],
                device_id={"seq": source, "chan": jnp.int32(slot % chans)},
            ).wait_recv()

    pieces = recv_f[...].astype(jnp.float32).reshape(per_chan, chans, own, LANES)
    total = jnp.sum(pieces, axis=1).reshape(per_chan * own, LANES)
    filter_out[...] = jnp.transpose(total) * scale

    for copy in sent:
        copy.wait_send()

    @pl.when(section > 0)
    def _():
        shift.wait_send()

    for off in order:
        deliver(off).wait_send()

    @pl.when(jnp.logical_not(keeps_own))
    def _():
        deliver(0).wait_send()


def body(mesh, saved_input, pre_gate, post_gate, grad_held, loss_grad, filters, skip_gain):
    sections, n, chans = (mesh.shape[axis] for axis in ("section", "seq", "chan"))
    ticks, rows, width = saved_input.shape[1:]
    own = width // n
    length = rows * n
    scale = 1.0 / math.sqrt(length * chans * ticks)
    pair = pltpu.VMEM((n, 2, own, rows), jnp.bfloat16)
    single = pltpu.VMEM((n, own, rows), jnp.bfloat16)
    vmem = pl.BlockSpec(memory_space=pltpu.VMEM)
    gradient, lag_grad = pl.pallas_call(
        functools.partial(kernel, sections, n, chans, scale),
        out_shape=(
            jax.ShapeDtypeStruct((rows, width), jnp.bfloat16),
            jax.ShapeDtypeStruct((rows, width // chans), jnp.float32),
        ),
        in_specs=[vmem] * 7,
        out_specs=(vmem, vmem),
        scratch_shapes=[
            pair,
            pair,
            pair,
            pair,
            single,
            single,
            single,
            single,
            single,
            single,
            single,
            single,
            pltpu.VMEM((rows, width), jnp.bfloat16),
            pltpu.VMEM((rows, width), jnp.bfloat16),
            pltpu.VMEM((rows, width), jnp.float32),
            pltpu.VMEM((own, n, rows), jnp.float32),
            pltpu.VMEM((own, 2 * n, rows), jnp.float32),
            pltpu.VMEM((3, own, n, length), jnp.bfloat16),
            pltpu.VMEM((own, length, rows), jnp.bfloat16),
            pltpu.VMEM((own, n, rows), jnp.float32),
            pltpu.VMEM((own, n, rows), jnp.float32),
            pltpu.SemaphoreType.DMA((6, n)),
            pltpu.SemaphoreType.DMA((6, n)),
            pltpu.SemaphoreType.DMA((2,)),
        ],
        compiler_params=pltpu.CompilerParams(
            collective_id=0, has_side_effects=True, vmem_limit_bytes=48 * 1024 * 1024
        ),
    )(
        saved_input[0],
        pre_gate[0],
        post_gate[0],
        grad_held[0],
        loss_grad,
        filters[0],
        skip_gain,
    )
    return gradient[None], lag_grad[None]


def solution(mesh):
    placed = (
        P("section", None, "seq", "chan"),
        P("section", None, "seq", "chan"),
        P("section", None, "seq", "chan"),
        P("section", "seq", "chan"),
        P("seq", "chan"),
        P("section", "seq", None),
        P("section", None),
    )
    return jax.shard_map(
        functools.partial(body, mesh),
        mesh=mesh,
        in_specs=placed,
        out_specs=(P("section", "seq", "chan"), P("section", "seq", "chan")),
        check_vma=False,
    )
```

```python
import functools
import math

import jax
import jax.numpy as jnp
from jax import lax
from jax.experimental import pallas as pl
from jax.experimental.pallas import tpu as pltpu
from jax.sharding import PartitionSpec as P

LANES = 128


def kernel(
    sections,
    n,
    chans,
    scale,
    saved_hbm,
    pre_hbm,
    post_hbm,
    grad_hbm,
    loss_hbm,
    filters_hbm,
    gain_hbm,
    grad_out,
    filter_out,
    saved,
    pre,
    post,
    grad_held,
    loss_grad,
    filters,
    gain,
    send_a,
    recv_a,
    send_b,
    recv_b,
    send_c,
    recv_c,
    send_l,
    send_p,
    recv_p,
    send_d,
    recv_d,
    send_e,
    recv_e,
    send_f,
    recv_f,
    send_g,
    recv_g,
    gain_rows,
    rows,
    padded,
    left,
    hankel,
    result,
    load_sem,
    send_sem,
    recv_sem,
    shift_sem,
):
    section = lax.axis_index("section")
    me = lax.axis_index("seq")
    chan = lax.axis_index("chan")
    width = grad_held.shape[1]
    own = width // n
    per_chan = n // chans
    owner_chan = me // per_chan
    keeps_own = owner_chan == chan
    is_first = section == 0
    is_last = section == sections - 1
    order = sorted(range(1, n), key=lambda off: -min(off, n - off))

    barrier = pltpu.get_barrier_semaphore()
    for off in order:
        pl.semaphore_signal(barrier, inc=1, device_id={"seq": lax.rem(me + off, n)})

    @pl.when(jnp.logical_not(is_last))
    def _():
        pl.semaphore_signal(barrier, inc=1, device_id={"section": section + 1})

    def is_own(slot):
        return (chan * per_chan + slot // chans == me) & (slot % chans == chan)

    def origin(slot):
        return {"seq": chan * per_chan + slot // chans, "chan": jnp.int32(slot % chans)}

    for slot in range(n):

        @pl.when(jnp.logical_not(is_own(slot)))
        def _():
            pl.semaphore_signal(barrier, inc=1, device_id=origin(slot))

    loads = [
        pltpu.make_async_copy(src, dst, load_sem.at[index])
        for index, (src, dst) in enumerate(
            [
                (post_hbm, post),
                (grad_hbm, grad_held),
                (filters_hbm, filters),
                (pre_hbm, pre),
                (saved_hbm, saved),
                (gain_hbm, gain),
                (loss_hbm, loss_grad),
            ]
        )
    ]
    for load in loads:
        load.start()

    row_index = lax.broadcasted_iota(jnp.int32, (LANES, LANES), 0)
    lane_index = lax.broadcasted_iota(jnp.int32, (LANES, LANES), 1)
    flip = (row_index + lane_index == LANES - 1).astype(jnp.bfloat16)
    keep = lane_index <= row_index
    padded[:, n:, :] = jnp.zeros((own, n, LANES), jnp.float32)

    def by_channel(values):
        turned = jnp.transpose(values.astype(jnp.float32)).astype(jnp.bfloat16)
        return turned.reshape(n, own, LANES)

    def flipped(values):
        turned = jnp.transpose(values).astype(jnp.bfloat16)
        turned = jnp.dot(turned, flip, preferred_element_type=jnp.float32)
        return turned.astype(jnp.bfloat16).reshape(n, own, LANES)

    loads[0].wait()
    loads[1].wait()
    gated_0 = post[0].astype(jnp.float32) * grad_held[...].astype(jnp.float32)
    send_a[:, 0] = by_channel(gated_0)
    loads[2].wait()
    send_a[:, 1] = flipped(filters[...])
    loads[3].wait()
    send_b[:, 0] = by_channel(grad_held[...])
    send_b[:, 1] = by_channel(pre[0])
    send_c[...] = by_channel(post[1])
    send_p[...] = by_channel(pre[1])
    loads[4].wait()
    for tick in range(2):
        mixed = pre[tick].astype(jnp.float32) * saved[tick].astype(jnp.float32)
        send_d[:, tick] = flipped(mixed)
    loads[5].wait()
    gain_rows[...] = jnp.transpose(jnp.broadcast_to(gain[...], (LANES, width)))
    loads[6].wait()

    @pl.when(is_last)
    def _():
        send_l[...] = by_channel(loss_grad[...])

    def to_peer(src, dst, phase, off):
        peer = lax.rem(me + off, n)
        return pltpu.make_async_remote_copy(
            src_ref=src.at[peer],
            dst_ref=dst.at[me],
            send_sem=send_sem.at[phase, off],
            recv_sem=recv_sem.at[phase, off],
            device_id={"seq": peer},
        )

    def exchange(src, dst, phase):
        for off in order:
            to_peer(src, dst, phase, off).start()
        dst[me] = src[me]

    def arrive(src, dst, phase):
        for off in order:
            to_peer(src, dst, phase, off).wait_recv()

    def leave(src, dst, phase):
        for off in order:
            to_peer(src, dst, phase, off).wait_send()

    waiting = (
        n
        - 1
        + n
        + jnp.logical_not(is_first).astype(jnp.int32)
        - keeps_own.astype(jnp.int32)
    )
    pl.semaphore_wait(barrier, waiting)

    exchange(send_a, recv_a, 0)
    exchange(send_b, recv_b, 1)
    exchange(send_c, recv_c, 2)

    @pl.when(is_last)
    def _():
        exchange(send_l, recv_g, 3)

    exchange(send_p, recv_p, 4)
    exchange(send_d, recv_d, 5)

    def build_left(block, which):
        for m in range(n):
            padded[:, n - 1 - m, :] = block(m).astype(jnp.float32)

        def one(ch, carry):
            for m in range(n):
                left[which, ch, :, m * LANES : (m + 1) * LANES] = padded[
                    ch, n - 1 - m : 2 * n - 1 - m, :
                ].astype(jnp.bfloat16)
            return carry

        lax.fori_loop(0, own, one, 0)

    def correlate(tick):
        def one(ch, carry):
            held = rows[ch]

            def turned(m):
                spread = jnp.broadcast_to(held[m : m + 1], (LANES, LANES))
                return pltpu.roll(spread, 1, 1, stride=1, stride_axis=0)

            now = turned(0)
            for m in range(n):
                later = turned(m + 1) if m + 1 < n else jnp.zeros_like(now)
                hankel[tick, ch, m * LANES : (m + 1) * LANES, :] = jnp.where(
                    keep, now, later
                ).astype(jnp.bfloat16)
                now = later
            result[ch] = jnp.dot(
                left[0, ch], hankel[tick, ch], preferred_element_type=jnp.float32
            )
            return carry

        lax.fori_loop(0, own, one, 0)

    def lag_products():
        def one(ch, carry):
            result[ch] = jnp.dot(
                left[1, ch], hankel[0, ch], preferred_element_type=jnp.float32
            ) + jnp.dot(left[2, ch], hankel[1, ch], preferred_element_type=jnp.float32)
            return carry

        lax.fori_loop(0, own, one, 0)

    my_gain = gain_rows[pl.ds(pl.multiple_of(me * own, own), own), :]

    def combined(held, gate, gated, m):
        inner = result[:, m, :] + my_gain * gated
        total = held.astype(jnp.float32) + gate.astype(jnp.float32) * inner
        return total.astype(jnp.bfloat16)

    arrive(send_a, recv_a, 0)
    for m in range(n):
        rows[:, m, :] = recv_a[m, 0].astype(jnp.float32)
    build_left(lambda m: recv_a[m, 1], 0)
    correlate(0)
    arrive(send_b, recv_b, 1)
    for m in range(n):
        send_g[m] = combined(recv_b[m, 0], recv_b[m, 1], recv_a[m, 0].astype(jnp.float32), m)
    shift = pltpu.make_async_remote_copy(
        src_ref=send_g,
        dst_ref=recv_g,
        send_sem=shift_sem.at[0],
        recv_sem=shift_sem.at[1],
        device_id={"section": lax.rem(section + sections - 1, sections)},
    )

    @pl.when(jnp.logical_not(is_first))
    def _():
        shift.start()

    arrive(send_c, recv_c, 2)

    @pl.when(jnp.logical_not(is_last))
    def _():
        shift.wait_recv()

    @pl.when(is_last)
    def _():
        arrive(send_l, recv_g, 3)

    for m in range(n):
        rows[:, m, :] = recv_c[m].astype(jnp.float32) * recv_g[m].astype(jnp.float32)
    correlate(1)
    arrive(send_p, recv_p, 4)
    for m in range(n):
        send_e[m] = combined(recv_g[m], recv_p[m], rows[:, m, :], m)
    exchange(send_e, recv_e, 6)
    arrive(send_d, recv_d, 5)
    build_left(lambda m: recv_d[m, 0], 1)
    build_left(lambda m: recv_d[m, 1], 2)
    lag_products()
    for m in range(n):
        send_f[m] = result[:, m, :].astype(jnp.bfloat16)

    landing = lax.rem(me, per_chan) * chans + chan

    def deliver(off):
        target = lax.rem(me + off, n)
        return pltpu.make_async_remote_copy(
            src_ref=send_f.at[target],
            dst_ref=recv_f.at[landing],
            send_sem=send_sem.at[7, off],
            recv_sem=recv_sem.at[7, landing],
            device_id={"seq": target, "chan": owner_chan},
        )

    for off in order:
        deliver(off).start()

    @pl.when(jnp.logical_not(keeps_own))
    def _():
        deliver(0).start()

    @pl.when(keeps_own)
    def _():
        recv_f[landing] = send_f[me]

    arrive(send_e, recv_e, 6)
    gradient = recv_e[...].astype(jnp.float32).reshape(width, LANES)
    grad_out[...] = jnp.transpose(gradient).astype(jnp.bfloat16)

    leave(send_a, recv_a, 0)
    leave(send_b, recv_b, 1)
    leave(send_c, recv_c, 2)

    @pl.when(is_last)
    def _():
        leave(send_l, recv_g, 3)

    leave(send_p, recv_p, 4)
    leave(send_d, recv_d, 5)
    leave(send_e, recv_e, 6)

    @pl.when(jnp.logical_not(is_first))
    def _():
        shift.wait_send()

    for slot in range(n):

        @pl.when(jnp.logical_not(is_own(slot)))
        def _():
            pltpu.make_async_remote_copy(
                src_ref=send_f.at[0],
                dst_ref=recv_f.at[slot],
                send_sem=send_sem.at[7, 0],
                recv_sem=recv_sem.at[7, slot],
                device_id=origin(slot),
            ).wait_recv()

    pieces = recv_f[...].astype(jnp.float32).reshape(per_chan, chans, own, LANES)
    filter_out[...] = jnp.sum(pieces, axis=1).reshape(per_chan * own, LANES) * scale

    for off in order:
        deliver(off).wait_send()

    @pl.when(jnp.logical_not(keeps_own))
    def _():
        deliver(0).wait_send()


def body(mesh, saved_input, pre_gate, post_gate, grad_held, loss_grad, filters, skip_gain):
    sections, n, chans = (mesh.shape[axis] for axis in ("section", "seq", "chan"))
    ticks, rows, width = saved_input.shape[1:]
    own = width // n
    length = rows * n
    scale = 1.0 / math.sqrt(length * chans * ticks)
    pair = pltpu.VMEM((n, 2, own, rows), jnp.bfloat16)
    single = pltpu.VMEM((n, own, rows), jnp.bfloat16)
    both = pltpu.VMEM((ticks, rows, width), jnp.bfloat16)
    block = pltpu.VMEM((rows, width), jnp.bfloat16)
    vmem = pl.BlockSpec(memory_space=pltpu.VMEM)
    hbm = pl.BlockSpec(memory_space=pltpu.HBM)
    gradient, lag_grad = pl.pallas_call(
        functools.partial(kernel, sections, n, chans, scale),
        out_shape=(
            jax.ShapeDtypeStruct((rows, width), jnp.bfloat16),
            jax.ShapeDtypeStruct((width // chans, rows), jnp.float32),
        ),
        in_specs=[hbm] * 7,
        out_specs=(vmem, vmem),
        scratch_shapes=[both] * 3
        + [block] * 2
        + [
            pltpu.VMEM((rows, width), jnp.float32),
            pltpu.VMEM((1, width), jnp.float32),
        ]
        + [pair] * 4
        + [single] * 5
        + [pair] * 2
        + [single] * 6
        + [
            pltpu.VMEM((width, rows), jnp.float32),
            pltpu.VMEM((own, n, rows), jnp.float32),
            pltpu.VMEM((own, 2 * n, rows), jnp.float32),
            pltpu.VMEM((3, own, n, length), jnp.bfloat16),
            pltpu.VMEM((ticks, own, length, rows), jnp.bfloat16),
            pltpu.VMEM((own, n, rows), jnp.float32),
            pltpu.SemaphoreType.DMA((7,)),
            pltpu.SemaphoreType.DMA((8, n)),
            pltpu.SemaphoreType.DMA((8, n)),
            pltpu.SemaphoreType.DMA((2,)),
        ],
        compiler_params=pltpu.CompilerParams(
            collective_id=0, has_side_effects=True, vmem_limit_bytes=67_043_328
        ),
    )(
        saved_input[0],
        pre_gate[0],
        post_gate[0],
        grad_held[0],
        loss_grad,
        filters[0],
        skip_gain,
    )
    return gradient[None], jnp.transpose(lag_grad)[None]


def solution(mesh):
    placed = (
        P("section", None, "seq", "chan"),
        P("section", None, "seq", "chan"),
        P("section", None, "seq", "chan"),
        P("section", "seq", "chan"),
        P("seq", "chan"),
        P("section", "seq", None),
        P("section", None),
    )
    return jax.shard_map(
        functools.partial(body, mesh),
        mesh=mesh,
        in_specs=placed,
        out_specs=(P("section", "seq", "chan"), P("section", "seq", "chan")),
        check_vma=False,
    )
```

```python
import functools
import math

import jax
import jax.numpy as jnp
from jax import lax
from jax.experimental import pallas as pl
from jax.experimental.pallas import tpu as pltpu
from jax.sharding import PartitionSpec as P

LANES = 128


def kernel(
    sections,
    n,
    chans,
    scale,
    saved_hbm,
    pre_hbm,
    post_hbm,
    grad_hbm,
    loss_hbm,
    filters_hbm,
    gain_hbm,
    grad_out,
    filter_out,
    saved,
    pre,
    post,
    grad_held,
    loss_grad,
    filters,
    gain,
    send_a,
    recv_a,
    send_b,
    recv_b,
    send_c,
    recv_c,
    send_p,
    recv_p,
    send_d,
    recv_d,
    send_e,
    recv_e,
    send_f,
    recv_f,
    send_g,
    recv_g,
    gain_rows,
    rows,
    padded,
    left,
    hankel,
    result,
    load_sem,
    send_sem,
    recv_sem,
    shift_sem,
):
    section = lax.axis_index("section")
    me = lax.axis_index("seq")
    chan = lax.axis_index("chan")
    width = grad_held.shape[1]
    own = width // n
    per_chan = n // chans
    owner_chan = me // per_chan
    keeps_own = owner_chan == chan
    is_first = section == 0
    is_last = section == sections - 1
    order = sorted(range(1, n), key=lambda off: -min(off, n - off))

    barrier = pltpu.get_barrier_semaphore()
    for off in order:
        pl.semaphore_signal(barrier, inc=1, device_id={"seq": lax.rem(me + off, n)})

    @pl.when(jnp.logical_not(is_last))
    def _():
        pl.semaphore_signal(barrier, inc=1, device_id={"section": section + 1})

    def is_own(slot):
        return (chan * per_chan + slot // chans == me) & (slot % chans == chan)

    def origin(slot):
        return {"seq": chan * per_chan + slot // chans, "chan": jnp.int32(slot % chans)}

    for slot in range(n):

        @pl.when(jnp.logical_not(is_own(slot)))
        def _():
            pl.semaphore_signal(barrier, inc=1, device_id=origin(slot))

    loads = [
        pltpu.make_async_copy(src, dst, load_sem.at[index])
        for index, (src, dst) in enumerate(
            [
                (post_hbm, post),
                (grad_hbm, grad_held),
                (filters_hbm, filters),
                (pre_hbm, pre),
                (saved_hbm, saved),
                (gain_hbm, gain),
                (loss_hbm, loss_grad),
            ]
        )
    ]
    for load in loads:
        load.start()

    row_index = lax.broadcasted_iota(jnp.int32, (LANES, LANES), 0)
    lane_index = lax.broadcasted_iota(jnp.int32, (LANES, LANES), 1)
    flip = (row_index + lane_index == LANES - 1).astype(jnp.bfloat16)
    keep = lane_index <= row_index
    padded[:, n:, :] = jnp.zeros((own, n, LANES), jnp.float32)

    def by_channel(values):
        turned = jnp.transpose(values.astype(jnp.float32)).astype(jnp.bfloat16)
        return turned.reshape(n, own, LANES)

    def flipped(values):
        turned = jnp.transpose(values).astype(jnp.bfloat16)
        turned = jnp.dot(turned, flip, preferred_element_type=jnp.float32)
        return turned.astype(jnp.bfloat16).reshape(n, own, LANES)

    loads[0].wait()
    loads[1].wait()
    gated_0 = post[0].astype(jnp.float32) * grad_held[...].astype(jnp.float32)
    send_a[:, 0] = by_channel(gated_0)
    loads[2].wait()
    send_a[:, 1] = flipped(filters[...])
    loads[3].wait()
    send_b[:, 0] = by_channel(grad_held[...])
    send_b[:, 1] = by_channel(pre[0])
    send_p[...] = by_channel(pre[1])
    loads[4].wait()
    for tick in range(2):
        mixed = pre[tick].astype(jnp.float32) * saved[tick].astype(jnp.float32)
        send_d[:, tick] = flipped(mixed)
    loads[5].wait()
    gain_rows[...] = jnp.transpose(jnp.broadcast_to(gain[...], (LANES, width)))
    loads[6].wait()

    @pl.when(is_last)
    def _():
        held = loss_grad[...].astype(jnp.float32)
        send_c[...] = by_channel(post[1].astype(jnp.float32) * held)

    @pl.when(jnp.logical_not(is_last))
    def _():
        send_c[...] = by_channel(post[1])

    def to_peer(src, dst, phase, off):
        peer = lax.rem(me + off, n)
        return pltpu.make_async_remote_copy(
            src_ref=src.at[peer],
            dst_ref=dst.at[me],
            send_sem=send_sem.at[phase, off],
            recv_sem=recv_sem.at[phase, off],
            device_id={"seq": peer},
        )

    def exchange(src, dst, phase):
        for off in order:
            to_peer(src, dst, phase, off).start()
        dst[me] = src[me]

    def arrive(src, dst, phase):
        for off in order:
            to_peer(src, dst, phase, off).wait_recv()

    def leave(src, dst, phase):
        for off in order:
            to_peer(src, dst, phase, off).wait_send()

    waiting = (
        n
        - 1
        + n
        + jnp.logical_not(is_first).astype(jnp.int32)
        - keeps_own.astype(jnp.int32)
    )
    pl.semaphore_wait(barrier, waiting)

    exchange(send_a, recv_a, 0)
    exchange(send_b, recv_b, 1)
    exchange(send_c, recv_c, 2)


    @pl.when(jnp.logical_not(is_last))
    def _():
        exchange(send_p, recv_p, 4)

    exchange(send_d, recv_d, 5)

    def build_left(block, which):
        for m in range(n):
            padded[:, n - 1 - m, :] = block(m).astype(jnp.float32)

        def one(ch, carry):
            for m in range(n):
                left[which, ch, :, m * LANES : (m + 1) * LANES] = padded[
                    ch, n - 1 - m : 2 * n - 1 - m, :
                ].astype(jnp.bfloat16)
            return carry

        lax.fori_loop(0, own, one, 0, unroll=4)

    def correlate(tick):
        def one(ch, carry):
            held = rows[ch]

            def turned(m):
                spread = jnp.broadcast_to(held[m : m + 1], (LANES, LANES))
                return pltpu.roll(spread, 1, 1, stride=1, stride_axis=0)

            now = turned(0)
            for m in range(n):
                later = turned(m + 1) if m + 1 < n else jnp.zeros_like(now)
                hankel[tick, ch, m * LANES : (m + 1) * LANES, :] = jnp.where(
                    keep, now, later
                ).astype(jnp.bfloat16)
                now = later
            result[ch] = jnp.dot(
                left[0, ch], hankel[tick, ch], preferred_element_type=jnp.float32
            )
            return carry

        lax.fori_loop(0, own, one, 0, unroll=4)

    def lag_products():
        def one(ch, carry):
            result[ch] = jnp.dot(
                left[1, ch], hankel[0, ch], preferred_element_type=jnp.float32
            ) + jnp.dot(left[2, ch], hankel[1, ch], preferred_element_type=jnp.float32)
            return carry

        lax.fori_loop(0, own, one, 0, unroll=4)

    my_gain = gain_rows[pl.ds(pl.multiple_of(me * own, own), own), :]

    def combined(held, gate, gated, m):
        inner = result[:, m, :] + my_gain * gated
        total = held.astype(jnp.float32) + gate.astype(jnp.float32) * inner
        return total.astype(jnp.bfloat16)

    arrive(send_a, recv_a, 0)
    for m in range(n):
        rows[:, m, :] = recv_a[m, 0].astype(jnp.float32)
    build_left(lambda m: recv_a[m, 1], 0)
    correlate(0)
    arrive(send_b, recv_b, 1)
    for m in range(n):
        send_g[m] = combined(recv_b[m, 0], recv_b[m, 1], recv_a[m, 0].astype(jnp.float32), m)
    shift = pltpu.make_async_remote_copy(
        src_ref=send_g,
        dst_ref=recv_g,
        send_sem=shift_sem.at[0],
        recv_sem=shift_sem.at[1],
        device_id={"section": lax.rem(section + sections - 1, sections)},
    )

    @pl.when(jnp.logical_not(is_first))
    def _():
        shift.start()

    arrive(send_c, recv_c, 2)

    @pl.when(jnp.logical_not(is_last))
    def _():
        shift.wait_recv()
        for m in range(n):
            rows[:, m, :] = recv_c[m].astype(jnp.float32) * recv_g[m].astype(jnp.float32)

    @pl.when(is_last)
    def _():
        for m in range(n):
            rows[:, m, :] = recv_c[m].astype(jnp.float32)

    correlate(1)
    @pl.when(jnp.logical_not(is_last))
    def _():
        arrive(send_p, recv_p, 4)
        for m in range(n):
            send_e[m] = combined(recv_g[m], recv_p[m], rows[:, m, :], m)

    @pl.when(is_last)
    def _():
        for m in range(n):
            send_e[m] = result[:, m, :].astype(jnp.bfloat16)

    exchange(send_e, recv_e, 6)
    arrive(send_d, recv_d, 5)
    build_left(lambda m: recv_d[m, 0], 1)
    build_left(lambda m: recv_d[m, 1], 2)
    lag_products()
    for m in range(n):
        send_f[m] = result[:, m, :].astype(jnp.bfloat16)

    landing = lax.rem(me, per_chan) * chans + chan

    def deliver(off):
        target = lax.rem(me + off, n)
        return pltpu.make_async_remote_copy(
            src_ref=send_f.at[target],
            dst_ref=recv_f.at[landing],
            send_sem=send_sem.at[7, off],
            recv_sem=recv_sem.at[7, landing],
            device_id={"seq": target, "chan": owner_chan},
        )

    for off in order:
        deliver(off).start()

    @pl.when(jnp.logical_not(keeps_own))
    def _():
        deliver(0).start()

    @pl.when(keeps_own)
    def _():
        recv_f[landing] = send_f[me]

    arrive(send_e, recv_e, 6)
    back = jnp.transpose(recv_e[...].astype(jnp.float32).reshape(width, LANES))

    @pl.when(jnp.logical_not(is_last))
    def _():
        grad_out[...] = back.astype(jnp.bfloat16)

    @pl.when(is_last)
    def _():
        held = loss_grad[...].astype(jnp.float32)
        gated = post[1].astype(jnp.float32) * held
        inner = back + gain[...] * gated
        grad_out[...] = (held + pre[1].astype(jnp.float32) * inner).astype(jnp.bfloat16)

    leave(send_a, recv_a, 0)
    leave(send_b, recv_b, 1)
    leave(send_c, recv_c, 2)

    @pl.when(jnp.logical_not(is_last))
    def _():
        leave(send_p, recv_p, 4)

    leave(send_d, recv_d, 5)
    leave(send_e, recv_e, 6)

    @pl.when(jnp.logical_not(is_first))
    def _():
        shift.wait_send()

    for slot in range(n):

        @pl.when(jnp.logical_not(is_own(slot)))
        def _():
            pltpu.make_async_remote_copy(
                src_ref=send_f.at[0],
                dst_ref=recv_f.at[slot],
                send_sem=send_sem.at[7, 0],
                recv_sem=recv_sem.at[7, slot],
                device_id=origin(slot),
            ).wait_recv()

    pieces = recv_f[...].astype(jnp.float32).reshape(per_chan, chans, own, LANES)
    filter_out[...] = jnp.sum(pieces, axis=1).reshape(per_chan * own, LANES) * scale

    for off in order:
        deliver(off).wait_send()

    @pl.when(jnp.logical_not(keeps_own))
    def _():
        deliver(0).wait_send()


def body(mesh, saved_input, pre_gate, post_gate, grad_held, loss_grad, filters, skip_gain):
    sections, n, chans = (mesh.shape[axis] for axis in ("section", "seq", "chan"))
    ticks, rows, width = saved_input.shape[1:]
    own = width // n
    length = rows * n
    scale = 1.0 / math.sqrt(length * chans * ticks)
    pair = pltpu.VMEM((n, 2, own, rows), jnp.bfloat16)
    single = pltpu.VMEM((n, own, rows), jnp.bfloat16)
    both = pltpu.VMEM((ticks, rows, width), jnp.bfloat16)
    block = pltpu.VMEM((rows, width), jnp.bfloat16)
    vmem = pl.BlockSpec(memory_space=pltpu.VMEM)
    hbm = pl.BlockSpec(memory_space=pltpu.HBM)
    gradient, lag_grad = pl.pallas_call(
        functools.partial(kernel, sections, n, chans, scale),
        out_shape=(
            jax.ShapeDtypeStruct((rows, width), jnp.bfloat16),
            jax.ShapeDtypeStruct((width // chans, rows), jnp.float32),
        ),
        in_specs=[hbm] * 7,
        out_specs=(vmem, vmem),
        scratch_shapes=[both] * 3
        + [block] * 2
        + [
            pltpu.VMEM((rows, width), jnp.float32),
            pltpu.VMEM((1, width), jnp.float32),
        ]
        + [pair] * 4
        + [single] * 4
        + [pair] * 2
        + [single] * 6
        + [
            pltpu.VMEM((width, rows), jnp.float32),
            pltpu.VMEM((own, n, rows), jnp.float32),
            pltpu.VMEM((own, 2 * n, rows), jnp.float32),
            pltpu.VMEM((3, own, n, length), jnp.bfloat16),
            pltpu.VMEM((ticks, own, length, rows), jnp.bfloat16),
            pltpu.VMEM((own, n, rows), jnp.float32),
            pltpu.SemaphoreType.DMA((7,)),
            pltpu.SemaphoreType.DMA((8, n)),
            pltpu.SemaphoreType.DMA((8, n)),
            pltpu.SemaphoreType.DMA((2,)),
        ],
        compiler_params=pltpu.CompilerParams(
            collective_id=0, has_side_effects=True, vmem_limit_bytes=67_043_328
        ),
    )(
        saved_input[0],
        pre_gate[0],
        post_gate[0],
        grad_held[0],
        loss_grad,
        filters[0],
        skip_gain,
    )
    return gradient[None], jnp.transpose(lag_grad)[None]


def solution(mesh):
    placed = (
        P("section", None, "seq", "chan"),
        P("section", None, "seq", "chan"),
        P("section", None, "seq", "chan"),
        P("section", "seq", "chan"),
        P("seq", "chan"),
        P("section", "seq", None),
        P("section", None),
    )
    return jax.shard_map(
        functools.partial(body, mesh),
        mesh=mesh,
        in_specs=placed,
        out_specs=(P("section", "seq", "chan"), P("section", "seq", "chan")),
        check_vma=False,
    )
```
